128 devices in a mesh: seq: 16 (over x, y), head: 8 (over z, core).
Axes of the slice: x: 4, y: 4, z: 4, core: 2. Of those that a mesh axis runs over, the one named last changes fastest.
Arguments:
- head_inputs: bfloat16 [2, 8192, 8192], P(None, 'seq', 'head'), may hold values from -6 to 6
- gate_inputs: bfloat16 [2, 8192, 8192], P(None, 'seq', 'head'), may hold values from -6 to 6
- state_writes: bfloat16 [2, 8192, 1024], P(None, 'seq', 'head'), may hold values from -6 to 6
- state_reads: bfloat16 [2, 8192, 1024], P(None, 'seq', 'head'), may hold values from -6 to 6
- step_raw: float32 [2, 128, 8192], P(None, 'head', 'seq'), may hold values from -4 to 4
- decay_log: float32 [128], P('head')
- conv_inputs: float32 [4, 8192], P(None, 'head'), may hold values from -3 to 3
- conv_writes: float32 [4, 1024], P(None, 'head'), may hold values from -3 to 3
- conv_reads: float32 [4, 1024], P(None, 'head'), may hold values from -3 to 3
- norm_gain: float32 [8192], P('head'), may hold values from 0.1 to 1.9
- out_weight: bfloat16 [8192, 8192], P('head', 'seq'), may hold values from -0.0625 to 0.0625
Outputs:
- mixed: bfloat16 [2, 8192, 8192], P(None, 'seq', 'head')
The draws below stay inside these ranges and needn't reach their ends.
All inputs are finite; a program needn't handle non-finite values.
Results may differ from the reference program's by a relative error of at most 0.017.
Values may be sent and summed in bfloat16 or wider, within the bound.
No kernel may reach another device: no remote copies, remote signals or barrier semaphores. Data moves between devices by JAX's collectives and lax.ppermute only.
A program may use at most 128 MiB of HBM per device.

```python
import math
import jax
import jax.numpy as jnp
from jax import lax

D_MODEL = 8192
HEADS = 128
HEAD_DIM = 64
STATE = 128
GROUPS = 8
CONV = 4
SPAN = 128
SEQS = 2
INNER = 8192
LEN = 8192
N_HEAD = 8


def draw_decay_log(key, part):
    key_kind, key_slow, key_fast = jax.random.split(jax.random.fold_in(key, 11), 3)
    slow = jax.random.randint(key_kind, (HEADS,), 0, 2).astype(jnp.float32)
    slow_rate = jax.random.uniform(key_slow, (HEADS,), jnp.float32, math.log(0.3), math.log(2.0)) - jnp.log(jnp.float32(LEN))
    fast_rate = jax.random.uniform(key_fast, (HEADS,), jnp.float32, math.log(1.0 / 50.0), math.log(1.0 / 20.0))
    return slow * slow_rate + (1.0 - slow) * fast_rate


def shard_levels(stream_key, extent, cuts, smallest, high):
    level = 1.0
    for dim, blocks in cuts:
        heights = jax.random.uniform(jax.random.fold_in(jax.random.fold_in(stream_key, 6), dim), (blocks,), jnp.float32, smallest / len(cuts), high / len(cuts))
        level = level * jnp.repeat(jnp.exp(heights), extent[dim] // blocks).reshape((-1,) + (1,) * (len(extent) - 1 - dim))
    return level


def normal_values(rng, dims, spread, bound, shards=(), held_as=jnp.bfloat16):
    factor_of = shard_levels(rng, dims, shards, -0.22, 0.18) if shards else 1.0
    drawn = jax.random.normal(rng, dims, jnp.float32) * spread * factor_of
    return jnp.minimum(jnp.maximum(drawn, -bound), bound).astype(held_as)


def setup_inputs(seed: int = 0) -> dict:
    key_list = jax.random.split(jax.random.key(seed), 12)
    return {
        "head_inputs": normal_values(key_list[0], (SEQS, LEN, INNER), 1.0, 6.0, ((1, 16), (2, 8))),
        "gate_inputs": normal_values(key_list[1], (SEQS, LEN, INNER), 1.0, 6.0, ((1, 16), (2, 8))),
        "state_writes": normal_values(key_list[2], (SEQS, LEN, GROUPS * STATE), 1.0, 6.0, ((1, 16), (2, 8))),
        "state_reads": normal_values(key_list[3], (SEQS, LEN, GROUPS * STATE), 1.0, 6.0, ((1, 16), (2, 8))),
        "step_raw": normal_values(key_list[4], (SEQS, HEADS, LEN), 1.0, 4.0, ((1, 8), (2, 16)), jnp.float32),
        "decay_log": draw_decay_log(jax.random.fold_in(key_list[11], 71), 0),
        "conv_inputs": normal_values(key_list[6], (CONV, INNER), CONV ** -0.5, 3.0, ((1, 8),), jnp.float32),
        "conv_writes": normal_values(key_list[7], (CONV, GROUPS * STATE), CONV ** -0.5, 3.0, ((1, 8),), jnp.float32),
        "conv_reads": normal_values(key_list[8], (CONV, GROUPS * STATE), CONV ** -0.5, 3.0, ((1, 8),), jnp.float32),
        "norm_gain": jnp.clip(1.0 + 0.18 * jax.random.normal(key_list[9], (INNER,), jnp.float32), 0.1, 1.9),
        "out_weight": normal_values(key_list[10], (INNER, D_MODEL), INNER ** -0.5, 0.0625, ((0, 8), (1, 16))),
    }


HIGH = lax.Precision.HIGHEST

def causal_conv(seq_in, weight):
    length = seq_in.shape[1]
    joined = jnp.pad(seq_in.astype(jnp.float32), ((0, 0), (CONV - 1, 0), (0, 0)))
    total = weight[0] * joined[:, 0:length]
    for tap in range(1, CONV):
        total = total + weight[tap] * joined[:, tap:tap + length]
    return jax.nn.silu(total)

def reference(head_inputs, gate_inputs, state_writes, state_reads, step_raw, decay_log, conv_inputs, conv_writes, conv_reads, norm_gain, out_weight):
    per_group = HEADS // GROUPS
    spans = LEN // SPAN
    group_width = INNER // GROUPS
    values = causal_conv(head_inputs, conv_inputs)
    writes = causal_conv(state_writes, conv_writes)
    reads = causal_conv(state_reads, conv_reads)
    steps = jax.nn.softplus(step_raw)
    log_decay = steps * (-jnp.exp(decay_log))[None, :, None]
    later = jnp.arange(SPAN)[:, None] >= jnp.arange(SPAN)[None, :]

    def one_span(state, block):
        vals, wrs, rds, stp, logs, gate = block
        cumul = jnp.cumsum(logs, axis=-1)
        scores = jnp.einsum('ign,jgn->gij', rds, wrs, precision=HIGH)
        gaps = jnp.where(later, cumul[:, :, None] - cumul[:, None, :], -jnp.inf)
        mixing = (jnp.exp(gaps) * stp[:, None, :]).reshape(GROUPS, per_group, SPAN, SPAN) * scores[:, None]
        vals_g = vals.reshape(SPAN, GROUPS, per_group, HEAD_DIM)
        diag = jnp.einsum('ghij,jghp->ighp', mixing, vals_g, precision=HIGH)
        state_g = state.reshape(GROUPS, per_group, STATE, HEAD_DIM)
        scale_in = jnp.exp(cumul).reshape(GROUPS, per_group, SPAN).transpose(2, 0, 1)
        reading = jnp.einsum('ign,ghnp->ighp', rds, state_g, precision=HIGH) * scale_in[..., None]
        ssd = (diag + reading).reshape(SPAN, INNER)
        gated = ssd * jax.nn.silu(gate.astype(jnp.float32))
        grouped = gated.reshape(SPAN, GROUPS, group_width)
        normed = grouped * lax.rsqrt(lax.optimization_barrier(jnp.mean(grouped * grouped, axis=-1, keepdims=True)) + 1e-05)
        normed = (normed.reshape(SPAN, INNER) * norm_gain).astype(jnp.bfloat16)
        weights_in = (jnp.exp(cumul[:, -1:] - cumul) * stp).reshape(GROUPS, per_group, SPAN)
        fresh = jnp.einsum('jgn,ghj,jghp->ghnp', wrs, weights_in, vals_g, precision=HIGH).reshape(HEADS, STATE, HEAD_DIM)
        new_state = jnp.exp(cumul[:, -1])[:, None, None] * state + fresh
        return (new_state, normed)
    outputs = []
    for seq_index in range(SEQS):
        blocks = (values[seq_index].reshape(spans, SPAN, HEADS, HEAD_DIM), writes[seq_index].reshape(spans, SPAN, GROUPS, STATE), reads[seq_index].reshape(spans, SPAN, GROUPS, STATE), steps[seq_index].reshape(HEADS, spans, SPAN).transpose(1, 0, 2), log_decay[seq_index].reshape(HEADS, spans, SPAN).transpose(1, 0, 2), gate_inputs[seq_index].reshape(spans, SPAN, INNER))
        start = jnp.zeros((HEADS, STATE, HEAD_DIM), jnp.float32)
        final_state, normed = lax.scan(one_span, start, blocks)
        outputs.append(normed.reshape(LEN, INNER))
    rows = jnp.stack(outputs, axis=0).reshape(SEQS * LEN // SPAN, SPAN, INNER)
    block_width = INNER // N_HEAD

    def project_rows(row_block):
        total = jnp.zeros((SPAN, D_MODEL), jnp.float32)
        for index in range(N_HEAD):
            part = jnp.dot(row_block[:, index * block_width:(index + 1) * block_width], out_weight[index * block_width:(index + 1) * block_width], preferred_element_type=jnp.float32).astype(jnp.bfloat16)
            part = lax.optimization_barrier(part)
            total = total + part.astype(jnp.float32)
        return total.astype(jnp.bfloat16)
    mixed = lax.map(project_rows, rows)
    return mixed.reshape(SEQS, LEN, D_MODEL)
```

```python
import functools

import jax
import jax.numpy as jnp
from jax import lax
from jax.experimental import pallas as pl
from jax.experimental.pallas import tpu as pltpu
from jax.sharding import PartitionSpec as P

HEAD_DIM = 64
STATE = 128
CONV = 4
SPAN = 128
LOG2E = 1.4426950408889634
F32 = jnp.float32
BF16 = jnp.bfloat16
HIGH = lax.Precision.HIGHEST


def split(x):
    a = x.astype(BF16)
    r = x - a.astype(F32)
    b = r.astype(BF16)
    c = (r - b.astype(F32)).astype(BF16)
    return jnp.concatenate([a, b, c], axis=0)


def spread_matrix(heads, width):
    row = lax.broadcasted_iota(jnp.int32, (3 * heads, width), 0)
    col = lax.broadcasted_iota(jnp.int32, (3 * heads, width), 1)
    return (row % heads == col // HEAD_DIM).astype(BF16)


def spread(rows, matrix):
    return lax.dot_general(
        split(rows), matrix, (((0,), (0,)), ((), ())), preferred_element_type=F32
    )


def conv_silu(current, before, taps):
    n = current.shape[0]
    joined = jnp.concatenate([before, current], axis=0)
    half = (0.5 * taps[3:4]) * current
    for tap in range(CONV - 1):
        half = half + (0.5 * taps[tap : tap + 1]) * joined[5 + tap : 5 + tap + n]
    return half + half * jnp.tanh(half)


def decay_rows(step_ref, rate_ref):
    steps = jnp.log(1.0 + jnp.exp(step_ref[0]))
    logs = steps * (jnp.exp(rate_ref[...]) * (-LOG2E))
    i = lax.broadcasted_iota(jnp.int32, (SPAN, SPAN), 0)
    j = lax.broadcasted_iota(jnp.int32, (SPAN, SPAN), 1)
    upto = (i <= j).astype(F32)
    cumul = jnp.dot(logs, upto, precision=HIGH, preferred_element_type=F32)
    return steps, cumul


def state_kernel(
    heads_ref, writes_ref, reads_ref, halo_ref, step_ref, rate_ref, ci_ref, cw_ref, cr_ref,
    fed_ref, wr_ref, rd_ref, enter_ref, lead_ref, final_ref, total_ref,
    before, state, lead,
):
    span = pl.program_id(1)
    width = heads_ref.shape[2]
    nheads = width // HEAD_DIM

    @pl.when(span == 0)
    def _():
        before[...] = halo_ref[0].astype(F32)
        state[...] = jnp.zeros_like(state)
        lead[...] = jnp.zeros_like(lead)

    current = heads_ref[0].astype(F32)
    values = conv_silu(current, before[:, :width], ci_ref[...])
    before[:, :width] = current[SPAN - 8 :]
    current = writes_ref[0].astype(F32)
    writes = conv_silu(current, before[:, width : width + STATE], cw_ref[...]).astype(BF16)
    before[:, width : width + STATE] = current[SPAN - 8 :]
    wr_ref[0] = writes
    current = reads_ref[0].astype(F32)
    rd_ref[0] = conv_silu(current, before[:, width + STATE :], cr_ref[...]).astype(BF16)
    before[:, width + STATE :] = current[SPAN - 8 :]

    steps, cumul = decay_rows(step_ref, rate_ref)
    matrix = spread_matrix(nheads, width)
    fed_ref[0] = (values * spread(steps, matrix)).astype(BF16)
    last = cumul[:, SPAN - 1 :]
    kept = (values * spread(jnp.exp2(last - cumul) * steps, matrix)).astype(BF16)
    fresh = lax.dot_general(writes, kept, (((0,), (0,)), ((), ())), preferred_element_type=F32)
    block_log = spread(jnp.broadcast_to(last, (nheads, 8)), matrix)[0:1]
    enter_ref[0, 0] = state[...].astype(BF16)
    lead_ref[0, 0] = lead[...]
    state[...] = jnp.exp2(block_log) * state[...] + fresh
    lead[...] = lead[...] + block_log

    @pl.when(span == pl.num_programs(1) - 1)
    def _():
        final_ref[0] = state[...].astype(BF16)
        total_ref[0] = lead[...]


def diagonal_kernel(
    fed_ref, wr_ref, rd_ref, step_ref, rate_ref, gate_ref, part_ref, scale_ref
):
    width = fed_ref.shape[2]
    nheads = width // HEAD_DIM
    _, cumul = decay_rows(step_ref, rate_ref)
    columns = cumul.T
    scores = lax.dot_general(
        rd_ref[0], wr_ref[0], (((1,), (1,)), ((), ())), preferred_element_type=F32
    )
    i = lax.broadcasted_iota(jnp.int32, (SPAN, SPAN), 0)
    j = lax.broadcasted_iota(jnp.int32, (SPAN, SPAN), 1)
    scores = jnp.where(i >= j, scores, 0.0)
    half = 0.5 * gate_ref[0].astype(F32)
    gate = half + half * jnp.tanh(half)
    scale_ref[0] = spread(jnp.exp2(cumul), spread_matrix(nheads, width)) * gate
    first = lax.broadcasted_iota(jnp.int32, (SPAN, 2 * HEAD_DIM), 1) < HEAD_DIM
    for pair in range(nheads // 2):
        lanes = slice(pair * 2 * HEAD_DIM, (pair + 1) * 2 * HEAD_DIM)
        both = []
        for h in (2 * pair, 2 * pair + 1):
            gap = jnp.minimum(columns[:, h : h + 1] - cumul[h : h + 1, :], 0.0)
            both.append((jnp.exp2(gap) * scores).astype(BF16))
        out = jnp.dot(
            jnp.concatenate(both, axis=0), fed_ref[0, :, lanes], preferred_element_type=F32
        )
        part_ref[0, :, lanes] = jnp.where(first, out[:SPAN], out[SPAN:]) * gate[:, lanes]


def finish_kernel(
    part_ref, scale_ref, rd_ref, enter_ref, lead_ref, carried_ref, gain_ref, out_ref
):
    width = part_ref.shape[2]
    entering = enter_ref[0, 0].astype(F32) + jnp.exp2(lead_ref[0, 0]) * carried_ref[0].astype(F32)
    reading = jnp.dot(rd_ref[0], entering.astype(BF16), preferred_element_type=F32)
    gated = part_ref[0] + reading * scale_ref[0]
    mean = jnp.sum(gated * gated, axis=1, keepdims=True) * (1.0 / width)
    out_ref[0] = (gated * lax.rsqrt(mean + 1e-05) * gain_ref[...]).astype(BF16)


def carry_kernel(states_ref, logs_ref, out_ref):
    carried = jnp.zeros(states_ref.shape[1:], F32)
    for s in range(states_ref.shape[0]):
        out_ref[s] = carried.astype(BF16)
        carried = jnp.exp2(logs_ref[s]) * carried + states_ref[s].astype(F32)


def shape(dims, dtype):
    return jax.ShapeDtypeStruct(dims, dtype)


def call(kernel, name, interpret, **more):
    return pl.pallas_call(kernel, name=name, interpret=interpret, **more)


def per_device(
    interpret,
    head_inputs, gate_inputs, state_writes, state_reads, step_raw, decay_log,
    conv_inputs, conv_writes, conv_reads, norm_gain, out_weight,
):
    seqs, length, width = head_inputs.shape
    nheads = decay_log.shape[0]
    spans = length // SPAN
    devices = lax.axis_size("seq")
    place = lax.axis_index("seq")
    full_weight = lax.all_gather(out_weight, "seq", axis=1, tiled=True)

    rim = jnp.concatenate(
        [a[:, length - 8 :] for a in (head_inputs, state_writes, state_reads)], axis=2
    )
    halo = lax.ppermute(rim, "seq", [(k, k + 1) for k in range(devices - 1)])
    rate = decay_log[:, None]

    block = lambda c: pl.BlockSpec((1, SPAN, c), lambda s, k: (s, k, 0))
    rows = pl.BlockSpec((1, nheads, SPAN), lambda s, k: (s, 0, k))
    whole = lambda a: pl.BlockSpec(a.shape, lambda s, k: (0,) * a.ndim)
    each = lambda r, c: pl.BlockSpec((1, r, c), lambda s, k: (s, 0, 0))
    stack = lambda r, c: pl.BlockSpec((1, 1, r, c), lambda s, k: (s, k, 0, 0))
    taps = (conv_inputs, conv_writes, conv_reads)
    fed, writes, reads, enter, lead, final, total = call(
        state_kernel, "state", interpret,
        grid=(seqs, spans),
        in_specs=[
            block(width), block(STATE), block(STATE), each(8, width + 2 * STATE), rows, whole(rate),
            *[whole(a) for a in taps],
        ],
        out_specs=[
            block(width), block(STATE), block(STATE), stack(STATE, width), stack(1, width),
            each(STATE, width), each(1, width),
        ],
        out_shape=[
            shape((seqs, length, width), BF16), shape((seqs, length, STATE), BF16),
            shape((seqs, length, STATE), BF16), shape((seqs, spans, STATE, width), BF16),
            shape((seqs, spans, 1, width), F32), shape((seqs, STATE, width), BF16),
            shape((seqs, 1, width), F32),
        ],
        scratch_shapes=[
            pltpu.VMEM((8, width + 2 * STATE), F32), pltpu.VMEM((STATE, width), F32),
            pltpu.VMEM((1, width), F32),
        ],
    )(head_inputs, state_writes, state_reads, halo, step_raw, rate, *taps)

    lanes = width // (devices // 2)
    pieces = final.reshape(seqs, 2, STATE // 2, devices // 2, lanes)
    pieces = pieces.transpose(3, 1, 0, 2, 4).reshape(devices, seqs, STATE // 2, lanes)
    a = total.astype(BF16)
    rest = total - a.astype(F32)
    b = rest.astype(BF16)
    c = (rest - b.astype(F32)).astype(BF16)
    logs = jnp.concatenate([a, b, c, jnp.zeros((seqs, 5, width), BF16)], axis=1)
    logs = logs.reshape(seqs, 8, devices // 2, lanes).transpose(2, 0, 1, 3)
    logs = jnp.repeat(logs, 2, axis=0)
    sent = jnp.concatenate([pieces, logs], axis=2)
    got = lax.all_to_all(sent, "seq", 0, 0)
    got_logs = jnp.sum(got[:, :, STATE // 2 :].astype(F32), axis=2, keepdims=True)
    ahead = call(
        carry_kernel, "carry", interpret, out_shape=shape((devices, seqs, STATE // 2, lanes), BF16)
    )(got[:, :, : STATE // 2], got_logs)
    back = lax.all_to_all(ahead, "seq", 0, 0)
    carried = back.reshape(devices // 2, 2, seqs, STATE // 2, lanes)
    carried = carried.transpose(2, 1, 3, 0, 4).reshape(seqs, STATE, width)

    part, scale = call(
        diagonal_kernel, "diagonal", interpret,
        grid=(seqs, spans),
        in_specs=[block(width), block(STATE), block(STATE), rows, whole(rate), block(width)],
        out_specs=[block(width), block(width)],
        out_shape=[shape((seqs, length, width), F32)] * 2,
    )(fed, writes, reads, step_raw, rate, gate_inputs)

    gain = norm_gain[None]
    normed = call(
        finish_kernel, "finish", interpret,
        grid=(seqs, spans),
        in_specs=[
            block(width), block(width), block(STATE), stack(STATE, width), stack(1, width),
            each(STATE, width), whole(gain),
        ],
        out_specs=block(width),
        out_shape=shape((seqs, length, width), BF16),
    )(part, scale, reads, enter, lead, carried, gain)

    partial_out = jnp.dot(
        normed.reshape(seqs * length, width), full_weight, preferred_element_type=F32
    )
    mixed = lax.psum_scatter(partial_out.astype(BF16), "head", scatter_dimension=1, tiled=True)
    return mixed.reshape(seqs, length, mixed.shape[1])


def solution(mesh, interpret=False):
    return jax.shard_map(
        functools.partial(per_device, interpret),
        mesh=mesh,
        in_specs=(
            P(None, "seq", "head"),
            P(None, "seq", "head"),
            P(None, "seq", "head"),
            P(None, "seq", "head"),
            P(None, "head", "seq"),
            P("head"),
            P(None, "head"),
            P(None, "head"),
            P(None, "head"),
            P("head"),
            P("head", "seq"),
        ),
        out_specs=P(None, "seq", "head"),
        check_vma=False,
    )
```
